32 devices in a mesh: row: 16 (over z, x, core), col: 2 (over y).
Axes of the slice: x: 2, y: 2, z: 4, core: 2. Of those that a mesh axis runs over, the one named last changes fastest.
Arguments:
- x_train: bfloat16 [64, 8192], P(None, 'col'), may hold values from -8 to 8
- targets: float32 [8192], P('col'), may hold values from -6 to 6
- noise_draws: float32 [8192, 256], P('col', 'row'), may hold values from -3 to 3
- alpha_init: float32 [8192, 256], P('col', 'row'), may hold values from -6 to 6
- velocity_init: float32 [8192, 256], P('col', 'row'), may hold values from -3 to 3
- frequencies: bfloat16 [64, 4096], P(None, 'col'), may hold values from -5 to 5
- phases: float32 [4096], P('col'), may hold values from -3.140625 to 3.140625
- path_weights: bfloat16 [4096, 256], P('col'), may hold values from -6 to 6
- x_window: bfloat16 [64, 32768], P(None, 'row'), may hold values from -6 to 6
- batch_index: int32 [3, 8192], replicated, may hold values from 0 to 8191, as said below
Outputs:
- alpha_out: float32 [8192, 256], P('col', 'row')
- velocity_out: float32 [8192, 256], P('col', 'row')
- prior_window: float32 [256, 32768], P('col', 'row')
The draws below stay inside these ranges and needn't reach their ends.
Inputs may be any that keep to these rules, and one draw needn't show every extreme that they name: `batch_index`: row b of every step names a training point of group g = (b // 256) % 2, that is a number from g * 4096 to (g + 1) * 4096 - 1; points may repeat.
All inputs are finite; a program needn't handle non-finite values.
Results may differ from the reference program's by a relative error of at most 0.0039.
Values may be sent and summed in bfloat16 or wider, within the bound.
A program may use at most 64 MiB of HBM per device.

```python
import jax
import jax.numpy as jnp
from jax import lax

D_IN = 64
FEAT = 4096
PATHS = 256
STEPS = 3
TRAIN_DEV = 4096
BATCH_DEV = 512
WINDOW_DEV = 2048
TRAIN = 8192
BATCH = 8192
WINDOW = 32768
N_ROW = 16


def draw_x_train(key, part):
    clusters = max(TRAIN // 4, 1)
    center_scale = (40.0 / D_IN) ** 0.5
    offset_scale = (1.0 / D_IN) ** 0.5
    member = jax.random.randint(jax.random.fold_in(key, 14), (TRAIN,), 0, clusters)
    center_key = jax.random.fold_in(key, 15)
    offset_key = jax.random.fold_in(key, 16)
    centers = center_scale * jax.random.normal(center_key, (D_IN, clusters), jnp.float32)
    offsets = offset_scale * jax.random.normal(offset_key, (D_IN, TRAIN), jnp.float32)
    points = jnp.take(centers, member, axis=1) + offsets
    return jnp.clip(points, -8.0, 8.0).astype(jnp.bfloat16)


def draw_batch_index(key, part):
    col_groups = TRAIN // TRAIN_DEV
    own_rows = BATCH_DEV // col_groups
    positions = jnp.arange(BATCH)
    group_ids = positions // own_rows % col_groups
    offsets = jax.random.randint(jax.random.fold_in(key, 21), (STEPS, BATCH), 0, TRAIN_DEV)
    return (group_ids[None, :] * TRAIN_DEV + offsets).astype(jnp.int32)


def level_of(key, shape, cuts, smallest, top_value):
    loudness = 1.0
    for position, shards_of in cuts:
        steps = jax.random.uniform(jax.random.fold_in(jax.random.fold_in(key, 6), position), (shards_of,), jnp.float32, smallest / len(cuts), top_value / len(cuts))
        loudness = loudness * jnp.repeat(jnp.exp(steps), shape[position] // shards_of).reshape((-1,) + (1,) * (len(shape) - 1 - position))
    return loudness


def gaussian(rng, extent, deviation, most, pieces=(), kind=jnp.bfloat16):
    entries = deviation * jax.random.normal(rng, extent, jnp.float32)
    if pieces:
        entries = entries * level_of(rng, extent, pieces, -0.22, 0.18)
    return jnp.clip(entries, -most, most).astype(kind)


def setup_inputs(seed: int = 0) -> dict:
    key_list = jax.random.split(jax.random.key(seed), 11)
    x_train = draw_x_train(jax.random.fold_in(key_list[10], 71), 0)
    targets = gaussian(key_list[1], (TRAIN,), 1.0, 6.0, ((0, 2),), jnp.float32)
    noise_draws = gaussian(key_list[2], (TRAIN, PATHS), 0.5, 3.0, ((0, 2), (1, 16)), jnp.float32)
    alpha_init = gaussian(key_list[3], (TRAIN, PATHS), 1.0, 6.0, ((0, 2), (1, 16)), jnp.float32)
    velocity_init = gaussian(key_list[4], (TRAIN, PATHS), 0.5, 3.0, ((0, 2), (1, 16)), jnp.float32)
    frequencies = gaussian(key_list[5], (D_IN, FEAT), 0.87, 5.0, ((1, 2),))
    phases = jnp.clip(jax.random.uniform(key_list[6], (FEAT,), jnp.float32, -3.140625, 3.140625), -3.140625, 3.140625)
    path_weights = gaussian(key_list[7], (FEAT, PATHS), 1.0, 6.0, ((0, 2),))
    x_window = gaussian(key_list[8], (D_IN, WINDOW), 1.0, 6.0, ((1, 16),))
    batch_index = draw_batch_index(jax.random.fold_in(key_list[10], 71), 0)
    return dict(x_train=x_train, targets=targets, noise_draws=noise_draws, alpha_init=alpha_init, velocity_init=velocity_init, frequencies=frequencies, phases=phases, path_weights=path_weights, x_window=x_window, batch_index=batch_index)


SQRT_THREE = 1.7320508075688772
LENGTH = 1.15
NOISE_VAR = 0.25
MOMENTUM = 0.9
STEP_SIZE = 0.5
HIGH = lax.Precision.HIGHEST

def features(points, frequencies, phases):
    phase_arg = jnp.dot(frequencies.astype(jnp.float32).T, points.astype(jnp.float32), precision=HIGH)
    factor = (2.0 / FEAT) ** 0.5
    return (factor * jnp.cos(phase_arg + phases[:, None])).astype(jnp.bfloat16)

def kernel_rows(points, x_train, train_norm):
    inner_prod = jnp.dot(points.astype(jnp.float32).T, x_train.astype(jnp.float32), precision=HIGH)
    point_norm = lax.optimization_barrier(jnp.sum(jnp.square(points.astype(jnp.float32)), axis=0))
    dist_sq = jnp.maximum(point_norm[:, None] + train_norm[None, :] - 2.0 * inner_prod, 0.0)
    scaled = SQRT_THREE / LENGTH * jnp.sqrt(dist_sq)
    return ((1.0 + scaled) * jnp.exp(-scaled)).astype(jnp.bfloat16)

def reference(x_train, targets, noise_draws, alpha_init, velocity_init, frequencies, phases, path_weights, x_window, batch_index):
    weights_wide = path_weights.astype(jnp.float32)
    window_blocks = x_window.reshape(D_IN, N_ROW, WINDOW_DEV).transpose(1, 0, 2)

    def window_block(points):
        phi_block = lax.optimization_barrier(features(points, frequencies, phases)).astype(jnp.float32)
        return jnp.dot(weights_wide.T, phi_block, precision=HIGH)
    prior_blocks = lax.map(window_block, window_blocks)
    prior_window = prior_blocks.transpose(1, 0, 2).reshape(PATHS, WINDOW)
    train_norm = lax.optimization_barrier(jnp.sum(jnp.square(x_train.astype(jnp.float32)), axis=0))
    block_rows = min(256, BATCH)
    alpha = alpha_init
    velocity = velocity_init
    for step_id in range(STEPS):
        index_now = batch_index[step_id].astype(jnp.int32)
        points = jnp.take(x_train, index_now, axis=1)
        coeffs = lax.optimization_barrier(alpha.astype(jnp.bfloat16)).astype(jnp.float32)
        point_blocks = points.reshape(D_IN, BATCH // block_rows, block_rows).transpose(1, 0, 2)

        def batch_block(block_points):
            kernel = lax.optimization_barrier(kernel_rows(block_points, x_train, train_norm)).astype(jnp.float32)
            coupled = jnp.dot(kernel, coeffs, precision=HIGH)
            phi_block = lax.optimization_barrier(features(block_points, frequencies, phases)).astype(jnp.float32)
            return coupled + jnp.dot(phi_block.T, weights_wide, precision=HIGH)
        batch_sum = lax.map(batch_block, point_blocks).reshape(BATCH, PATHS)
        row_terms = batch_sum + NOISE_VAR * alpha[index_now] - targets[index_now][:, None] + noise_draws[index_now]
        gradient = jnp.zeros_like(alpha).at[index_now].add(row_terms)
        velocity = MOMENTUM * velocity - STEP_SIZE * gradient
        alpha = alpha + velocity
    return (alpha, velocity, prior_window)
```

```python
import functools

import jax
import jax.numpy as jnp
import numpy as np
from jax import lax
from jax.experimental import pallas as pl
from jax.experimental.pallas import tpu as pltpu
from jax.sharding import PartitionSpec as P

SQRT_THREE = 1.7320508075688772
LENGTH = 1.15
NOISE_VAR = 0.25
MOMENTUM = 0.9
STEP_SIZE = 0.5


def sine_coeffs(scale):
    nodes = 5
    k = np.arange(nodes)
    v = (np.cos((2 * k + 1) * np.pi / (2 * nodes)) + 1) / 2 / 16
    z = np.sqrt(v)
    q = np.sin(2 * np.pi * z) / z
    return [float(c * scale) for c in np.linalg.solve(np.vander(v, nodes, increasing=True), q)]


def scaled_cos(turns, coeffs):
    z = 0.25 - jnp.abs(turns - jnp.round(turns))
    v = z * z
    q = coeffs[-1]
    for c in coeffs[-2::-1]:
        q = q * v + c
    return q * z


def prior_kernel(coeffs, tile_f, freq_ref, phase_ref, weight_ref, point_ref, out_ref):
    feat = freq_ref.shape[0]
    points = point_ref[...]

    def body(i, acc):
        rows = pl.ds(pl.multiple_of(i * tile_f, tile_f), tile_f)
        arg = jnp.dot(freq_ref[rows, :], points, preferred_element_type=jnp.float32)
        turns = (arg + phase_ref[rows, :]) * (0.5 / np.pi)
        phi = scaled_cos(turns, coeffs).astype(jnp.bfloat16)
        return acc + lax.dot_general(
            weight_ref[rows, :], phi, (((0,), (0,)), ((), ())), preferred_element_type=jnp.float32
        )

    out_ref[...] = lax.fori_loop(0, feat // tile_f, body, jnp.zeros(out_ref.shape, jnp.float32))


def prior_sums(freq_t, phase_col, weights, points, total_feat):
    feat, d_in = freq_t.shape
    paths = weights.shape[1]
    n = points.shape[1]
    tile_n = min(512, n)
    coeffs = sine_coeffs((2.0 / total_feat) ** 0.5)
    return pl.pallas_call(
        functools.partial(prior_kernel, coeffs, min(256, feat)),
        grid=(n // tile_n,),
        in_specs=[
            pl.BlockSpec((feat, d_in), lambda i: (0, 0)),
            pl.BlockSpec((feat, 1), lambda i: (0, 0)),
            pl.BlockSpec((feat, paths), lambda i: (0, 0)),
            pl.BlockSpec((d_in, tile_n), lambda i: (0, i)),
        ],
        out_specs=pl.BlockSpec((paths, tile_n), lambda i: (0, i)),
        out_shape=jax.ShapeDtypeStruct((paths, n), jnp.float32),
        cost_estimate=pl.CostEstimate(
            flops=2 * feat * n * (paths + d_in), bytes_accessed=4 * paths * n, transcendentals=feat * n
        ),
    )(freq_t, phase_col, weights, points)


def matern(points, train):
    inner = lax.dot_general(
        train, points, (((0,), (0,)), ((), ())), preferred_element_type=jnp.float32
    )
    point_norm = jnp.sum(jnp.square(points.astype(jnp.float32)), axis=0)
    train_norm = jnp.sum(jnp.square(train.astype(jnp.float32)), axis=0)
    dist_sq = jnp.maximum(train_norm[:, None] + point_norm[None, :] - 2.0 * inner, 0.0)
    scaled = SQRT_THREE / LENGTH * jnp.sqrt(dist_sq)
    return ((1.0 + scaled) * jnp.exp(-scaled)).astype(jnp.bfloat16)


def point_counts(index, start, count):
    lanes = 128
    local = index - start
    high = (local // lanes)[:, None, :] == lax.broadcasted_iota(
        jnp.int32, (1, count // lanes, 1), 1
    )
    low = (local % lanes)[:, None, :] == lax.broadcasted_iota(jnp.int32, (1, lanes, 1), 1)
    tables = lax.dot_general(
        high.astype(jnp.bfloat16),
        low.astype(jnp.bfloat16),
        (((2,), (2,)), ((0,), (0,))),
        preferred_element_type=jnp.float32,
    )
    return tables.reshape(index.shape[0], count)


def shards(
    x_train,
    targets,
    noise_draws,
    alpha_init,
    velocity_init,
    frequencies,
    phases,
    path_weights,
    x_window,
    batch_index,
):
    row_count = lax.axis_size("row")
    col_count = lax.axis_size("col")
    row_id = lax.axis_index("row")
    col_id = lax.axis_index("col")
    train_cols = x_train.shape[1]
    own = train_cols // row_count
    steps = batch_index.shape[0]
    total_feat = frequencies.shape[1] * col_count

    mine = lax.dynamic_slice_in_dim(x_train, row_id * own, own, 1)
    points = lax.all_gather(mine, "col", axis=1, tiled=True)
    freq_t = frequencies.T
    phase_col = phases[:, None]
    kernel_tile = matern(points, x_train)
    prior_rows = prior_sums(freq_t, phase_col, path_weights, points, total_feat)
    window = prior_sums(freq_t, phase_col, path_weights, x_window, total_feat)
    prior_window = lax.psum_scatter(window, "col", scatter_dimension=0, tiled=True)

    counts = point_counts(batch_index, col_id * train_cols, train_cols)
    base = (noise_draws - targets[:, None]).T
    dual, velocity = alpha_init.T, velocity_init.T
    for step in range(steps):
        coeffs = lax.all_gather(dual.astype(jnp.bfloat16), "row", axis=0, tiled=True)
        sums = jnp.dot(coeffs, kernel_tile, preferred_element_type=jnp.float32) + prior_rows
        mine_sums = lax.psum_scatter(sums, "col", scatter_dimension=1, tiled=True)
        arrived = lax.all_to_all(mine_sums, "row", split_axis=0, concat_axis=1, tiled=True)
        gradient = counts[step][None, :] * (arrived + NOISE_VAR * dual + base)
        velocity = MOMENTUM * velocity - STEP_SIZE * gradient
        dual = dual + velocity
    return (dual.T, velocity.T, prior_window)


def solution(mesh):
    placed = (
        P(None, "col"),
        P("col"),
        P("col", "row"),
        P("col", "row"),
        P("col", "row"),
        P(None, "col"),
        P("col"),
        P("col", None),
        P(None, "row"),
        P(),
    )
    return jax.shard_map(
        shards,
        mesh=mesh,
        in_specs=placed,
        out_specs=(P("col", "row"), P("col", "row"), P("col", "row")),
        check_vma=False,
    )
```

```python
import functools

import jax
import jax.numpy as jnp
import numpy as np
from jax import lax
from jax.experimental import pallas as pl
from jax.experimental.pallas import tpu as pltpu
from jax.sharding import PartitionSpec as P

SQRT_THREE = 1.7320508075688772
LENGTH = 1.15
NOISE_VAR = 0.25
MOMENTUM = 0.9
STEP_SIZE = 0.5


def sine_coeffs(scale):
    nodes = 5
    k = np.arange(nodes)
    v = (np.cos((2 * k + 1) * np.pi / (2 * nodes)) + 1) / 2 / 16
    z = np.sqrt(v)
    q = np.sin(2 * np.pi * z) / z
    return [float(c * scale) for c in np.linalg.solve(np.vander(v, nodes, increasing=True), q)]


def scaled_cos(turns, coeffs):
    z = 0.25 - jnp.abs(turns - jnp.round(turns))
    v = z * z
    q = coeffs[-1]
    for c in coeffs[-2::-1]:
        q = q * v + c
    return q * z


def prior_kernel(coeffs, tile_f, freq_ref, phase_ref, weight_ref, point_ref, out_ref):
    feat = freq_ref.shape[0]
    points = point_ref[...]

    def body(i, acc):
        rows = pl.ds(pl.multiple_of(i * tile_f, tile_f), tile_f)
        arg = jnp.dot(freq_ref[rows, :], points, preferred_element_type=jnp.float32)
        turns = (arg + phase_ref[rows, :]) * (0.5 / np.pi)
        phi = scaled_cos(turns, coeffs).astype(jnp.bfloat16)
        return acc + lax.dot_general(
            weight_ref[rows, :], phi, (((0,), (0,)), ((), ())), preferred_element_type=jnp.float32
        )

    out_ref[...] = lax.fori_loop(0, feat // tile_f, body, jnp.zeros(out_ref.shape, jnp.float32))


def prior_sums(freq_t, phase_col, weights, points, total_feat):
    feat, d_in = freq_t.shape
    paths = weights.shape[1]
    n = points.shape[1]
    tile_n = min(512, n)
    coeffs = sine_coeffs((2.0 / total_feat) ** 0.5)
    return pl.pallas_call(
        functools.partial(prior_kernel, coeffs, min(256, feat)),
        grid=(n // tile_n,),
        in_specs=[
            pl.BlockSpec((feat, d_in), lambda i: (0, 0)),
            pl.BlockSpec((feat, 1), lambda i: (0, 0)),
            pl.BlockSpec((feat, paths), lambda i: (0, 0)),
            pl.BlockSpec((d_in, tile_n), lambda i: (0, i)),
        ],
        out_specs=pl.BlockSpec((paths, tile_n), lambda i: (0, i)),
        out_shape=jax.ShapeDtypeStruct((paths, n), jnp.float32),
        cost_estimate=pl.CostEstimate(
            flops=2 * feat * n * (paths + d_in), bytes_accessed=4 * paths * n, transcendentals=feat * n
        ),
    )(freq_t, phase_col, weights, points)


def matern(points, train):
    inner = lax.dot_general(
        train, points, (((0,), (0,)), ((), ())), preferred_element_type=jnp.float32
    )
    point_norm = jnp.sum(jnp.square(points.astype(jnp.float32)), axis=0)
    train_norm = jnp.sum(jnp.square(train.astype(jnp.float32)), axis=0)
    dist_sq = jnp.maximum(train_norm[:, None] + point_norm[None, :] - 2.0 * inner, 0.0)
    scaled = SQRT_THREE / LENGTH * jnp.sqrt(dist_sq)
    return ((1.0 + scaled) * jnp.exp(-scaled)).astype(jnp.bfloat16)


def point_counts(index, start, count):
    lanes = 128
    local = index - start
    high = (local // lanes)[:, None, :] == lax.broadcasted_iota(
        jnp.int32, (1, count // lanes, 1), 1
    )
    low = (local % lanes)[:, None, :] == lax.broadcasted_iota(jnp.int32, (1, lanes, 1), 1)
    tables = lax.dot_general(
        high.astype(jnp.bfloat16),
        low.astype(jnp.bfloat16),
        (((2,), (2,)), ((0,), (0,))),
        preferred_element_type=jnp.float32,
    )
    return tables.reshape(index.shape[0], count)


def shards(
    x_train,
    targets,
    noise_draws,
    alpha_init,
    velocity_init,
    frequencies,
    phases,
    path_weights,
    x_window,
    batch_index,
):
    row_count = lax.axis_size("row")
    col_count = lax.axis_size("col")
    row_id = lax.axis_index("row")
    col_id = lax.axis_index("col")
    train_cols = x_train.shape[1]
    own = train_cols // row_count
    steps = batch_index.shape[0]
    total_feat = frequencies.shape[1] * col_count

    mine = lax.dynamic_slice_in_dim(x_train, row_id * own, own, 1)
    points = lax.all_gather(mine, "col", axis=1, tiled=True)
    freq_t = frequencies.T
    phase_col = phases[:, None]
    kernel_tile = matern(points, x_train)
    prior_rows = prior_sums(freq_t, phase_col, path_weights, points, total_feat)
    window = prior_sums(freq_t, phase_col, path_weights, x_window, total_feat)
    prior_window = lax.psum_scatter(window, "col", scatter_dimension=0, tiled=True)

    counts = point_counts(batch_index, col_id * train_cols, train_cols)
    base = (noise_draws - targets[:, None]).T
    dual, velocity = alpha_init.T, velocity_init.T
    for step in range(steps):
        coeffs = lax.all_gather(dual.astype(jnp.bfloat16), "row", axis=0, tiled=True)
        sums = jnp.dot(coeffs, kernel_tile, preferred_element_type=jnp.float32) + prior_rows
        mine_sums = lax.psum_scatter(sums, "col", scatter_dimension=1, tiled=True)
        arrived = lax.all_to_all(mine_sums, "row", split_axis=0, concat_axis=1, tiled=True)
        gradient = counts[step][None, :] * (arrived + NOISE_VAR * dual + base)
        velocity = MOMENTUM * velocity - STEP_SIZE * gradient
        dual = dual + velocity
    return (dual.T, velocity.T, prior_window)


MESH = pl.DeviceIdType.MESH


def fused_kernel(
    scale_coeffs, steps, rows, x_ref, target_ref, noise_ref, alpha_in, velocity_in, freq_ref,
    phase_ref, weight_ref, window_ref, count_ref, alpha_ref, velocity_ref, prior_ref,
    gathered, tile, train_prior, points, points_t, base, outboxes, arrivals, last_outbox, last_arrived,
    window_out, window_in,
    ring_send, ring_recv, pair_send, pair_recv, sum_send, sum_recv, misc_send, misc_recv,
):
    div, rem = lax.div, lax.rem
    row = lax.axis_index("row")
    col = lax.axis_index("col")
    peer = 1 - col
    devices = rows * 2
    flat = row * 2 + col
    paths = weight_ref.shape[0]
    share = paths // rows
    train = x_ref.shape[1]
    own = train // rows
    feat = freq_ref.shape[1]
    half = train // 2
    chips = rows // 2
    core = rem(row, 2)
    chip = div(row, 2)
    depth, side = div(chip, 2), rem(chip, 2)
    place = depth * (1 - side) + (chips - 1 - depth) * side

    def row_at(position, on_core):
        p = rem(position + 2 * chips, chips)
        back = div(p, chips // 2)
        return ((1 - back) * 2 * p + back * (2 * (chips - 1 - p) + 1)) * 2 + on_core

    def device(d):
        other = rem(flat + d, devices)
        return div(other, 2), rem(other, 2)

    barrier = pltpu.get_barrier_semaphore()

    def greet(d, carry):
        pl.semaphore_signal(barrier, inc=1, device_id=device(d), device_id_type=MESH)
        return carry

    lax.fori_loop(1, devices, greet, 0)

    def block(step, r, h):
        return gathered.at[
            step, pl.ds(pl.multiple_of(r * share, share), share), pl.ds(h * half, half)
        ]

    def whole_block(step, r):
        return gathered.at[step, pl.ds(pl.multiple_of(r * share, share), share), :]

    def ring_copy(step, way, k, h):
        sign = 1 - 2 * way
        ref = block(step, row_at(place - sign * k, core), h)
        return pltpu.make_async_remote_copy(
            src_ref=ref, dst_ref=ref,
            send_sem=ring_send.at[step, way, k, h], recv_sem=ring_recv.at[step, way, k, h],
            device_id=(row_at(place + sign, core), col), device_id_type=MESH,
        )

    def pair_copy(step, way, k, h):
        sign = 1 - 2 * way
        ref = block(step, row_at(place - sign * (k + 1), core), h)
        return pltpu.make_async_remote_copy(
            src_ref=ref, dst_ref=ref,
            send_sem=pair_send.at[step, way, k, h], recv_sem=pair_recv.at[step, way, k, h],
            device_id=(row + 1 - 2 * core, col), device_id_type=MESH,
        )

    def own_copy(step):
        ref = whole_block(step, row)
        return pltpu.make_async_remote_copy(
            src_ref=ref, dst_ref=ref,
            send_sem=misc_send.at[step], recv_sem=misc_recv.at[step],
            device_id=(row + 1 - 2 * core, col), device_id_type=MESH,
        )

    last = chips // 2 - 1

    def hops(action):
        def event(e, carry):
            k, h = div(e, 2), rem(e, 2)
            for way in (0, 1):
                @pl.when((k < last) | (h == way))
                def _():
                    action(way, k, h)
            return carry

        lax.fori_loop(0, 2 * (last + 1), event, 0)

    def gather(step, compute):
        gathered[step, pl.ds(pl.multiple_of(row * share, share), share), :] = alpha_ref[
            ...
        ].astype(jnp.bfloat16)
        for h in (0, 1):
            for way in (0, 1):
                ring_copy(step, way, 0, h).start()
        own_copy(step).start()

        def event(e, carry):
            compute(e)
            k, h = div(e, 2), rem(e, 2)
            for way in (0, 1):
                @pl.when((k < last) | (h == way))
                def _():
                    ring_copy(step, way, k, h).wait_recv()

                    @pl.when((k < last - 1) | ((k == last - 1) & (h == way)))
                    def _():
                        ring_copy(step, way, k + 1, h).start()

                    pair_copy(step, way, k, h).start()
            return carry

        lax.fori_loop(0, 2 * (last + 1), event, 0)
        own_copy(step).wait_recv()
        hops(lambda way, k, h: pair_copy(step, way, k, h).wait_recv())

    def boxes(step):
        if step < steps - 1:
            return outboxes.at[step], arrivals.at[step]
        return last_outbox, last_arrived

    def sum_copy(step, d):
        r, c = device(d)
        outbox, arrived = boxes(step)
        return pltpu.make_async_remote_copy(
            src_ref=outbox.at[
                pl.ds(pl.multiple_of(r * share, share), share),
                pl.ds(pl.multiple_of(c * own, own), own),
            ],
            dst_ref=arrived.at[col, :, pl.ds(pl.multiple_of(row * own, own), own)],
            send_sem=sum_send.at[step, d], recv_sem=sum_recv.at[step, d],
            device_id=(r, c), device_id_type=MESH,
        )

    def point_copy():
        return pltpu.make_async_remote_copy(
            src_ref=x_ref.at[:, pl.ds(pl.multiple_of(row * own, own), own)],
            dst_ref=points.at[col],
            send_sem=misc_send.at[steps], recv_sem=misc_recv.at[steps],
            device_id=(row, peer), device_id_type=MESH,
        )

    def window_copy(part):
        width = window_out.shape[2]
        return pltpu.make_async_remote_copy(
            src_ref=window_out.at[part], dst_ref=window_in.at[part],
            send_sem=misc_send.at[steps + 1 + part], recv_sem=misc_recv.at[steps + 1 + part],
            device_id=(row, peer), device_id_type=MESH,
        )

    alpha_ref[...] = alpha_in[...]
    velocity_ref[...] = velocity_in[...]
    base[...] = noise_ref[...] - target_ref[...]
    pl.semaphore_wait(barrier, devices - 1)
    point_copy().start()
    points[col] = x_ref[:, pl.ds(pl.multiple_of(row * own, own), own)]
    train_prior[...] = jnp.zeros_like(train_prior)
    events = 2 * (last + 1)

    def phi_block(pts_t, cols):
        arg = jnp.dot(pts_t, freq_ref[:, cols], preferred_element_type=jnp.float32)
        turns = (arg + phase_ref[:, cols]) * (0.5 / np.pi)
        return scaled_cos(turns, scale_coeffs).astype(jnp.bfloat16)

    def against(a, b):
        return lax.dot_general(
            a, b, (((1,), (1,)), ((), ())), preferred_element_type=jnp.float32
        )

    def train_work(e):
        @pl.when(e == 0)
        def _():
            point_copy().wait_recv()
            for c in (0, 1):
                points_t[c * own : (c + 1) * own, :] = points[c].astype(jnp.float32).T

        width = train // events
        cols = pl.ds(pl.multiple_of(e * width, width), width)
        trains = x_ref[:, cols]
        train_norm = jnp.sum(jnp.square(trains.astype(jnp.float32)), axis=0, keepdims=True)
        fwidth = feat // events
        fcols = pl.ds(pl.multiple_of(e * fwidth, fwidth), fwidth)
        group = 128

        def rows_of(i, carry):
            span = pl.ds(pl.multiple_of(i * group, group), group)
            pts = points_t[span, :]
            pts_norm = jnp.sum(jnp.square(pts), axis=1, keepdims=True)
            pts = pts.astype(jnp.bfloat16)
            inner = jnp.dot(pts, trains, preferred_element_type=jnp.float32)
            dist_sq = jnp.maximum(pts_norm + train_norm - 2.0 * inner, 0.0)
            scaled = SQRT_THREE / LENGTH * jnp.sqrt(dist_sq)
            tile[span, cols] = ((1.0 + scaled) * jnp.exp(-scaled)).astype(jnp.bfloat16)
            train_prior[:, span] += against(weight_ref[:, fcols], phi_block(pts, fcols))
            return carry

        lax.fori_loop(0, 2 * own // group, rows_of, 0)

    tiles = 2 * events
    wide = window_ref.shape[1] // tiles

    def window_work(part):
        def work(e):
            span = pl.ds(pl.multiple_of((part * events + e) * wide, wide), wide)
            pts = window_ref[:, span].astype(jnp.float32).T.astype(jnp.bfloat16)
            fwidth = min(512, feat)

            def feats(i, acc):
                fcols = pl.ds(pl.multiple_of(i * fwidth, fwidth), fwidth)
                return acc + against(weight_ref[:, fcols], phi_block(pts, fcols))

            acc = lax.fori_loop(
                0, feat // fwidth, feats, jnp.zeros((paths, wide), jnp.float32)
            )
            kept = paths // 2
            mine = jnp.where(col == 0, acc[:kept], acc[kept:])
            sent = jnp.where(col == 0, acc[kept:], acc[:kept])
            prior_ref[:, span] = mine
            window_out[part, :, pl.ds(pl.multiple_of(e * wide, wide), wide)] = sent.astype(
                jnp.bfloat16
            )

        return work

    for step in range(steps):
        if step == 0:
            gather(step, train_work)
        elif step < 3:
            gather(step, window_work(step - 1))
            window_copy(step - 1).start()
        else:
            gather(step, lambda e: None)
        outbox, arrived = boxes(step)
        for c in (0, 1):
            span = slice(c * own, (c + 1) * own)
            sums = against(gathered[step], tile[span, :]) + train_prior[:, span]
            outbox[:, span] = sums.astype(outbox.dtype)

        def send(d, carry):
            sum_copy(step, d).start()
            return carry

        lax.fori_loop(1, devices, send, 0)
        arrived[col, :, pl.ds(pl.multiple_of(row * own, own), own)] = outbox[
            pl.ds(pl.multiple_of(row * share, share), share),
            pl.ds(pl.multiple_of(col * own, own), own),
        ]

        def receive(d, carry):
            sum_copy(step, d).wait_recv()
            return carry

        lax.fori_loop(1, devices, receive, 0)
        total = arrived[0].astype(jnp.float32) + arrived[1].astype(jnp.float32)
        alpha = alpha_ref[...]
        gradient = count_ref[step : step + 1, :] * (total + NOISE_VAR * alpha + base[...])
        speed = MOMENTUM * velocity_ref[...] - STEP_SIZE * gradient
        velocity_ref[...] = speed
        alpha_ref[...] = alpha + speed

    for part in (0, 1):
        window_copy(part).wait()
        width = window_out.shape[2]
        span = slice(part * width, (part + 1) * width)
        prior_ref[:, span] = prior_ref[:, span] + window_in[part].astype(jnp.float32)
    point_copy().wait_send()
    for step in range(steps):
        own_copy(step).wait_send()
        hops(lambda way, k, h: ring_copy(step, way, k, h).wait_send())
        hops(lambda way, k, h: pair_copy(step, way, k, h).wait_send())

        def drain(d, carry):
            sum_copy(step, d).wait_send()
            return carry

        lax.fori_loop(1, devices, drain, 0)


def fused_shards(
    x_train, targets, noise_draws, alpha_init, velocity_init, frequencies, phases, path_weights,
    x_window, batch_index,
):
    rows = lax.axis_size("row")
    col_count = lax.axis_size("col")
    train = x_train.shape[1]
    steps = batch_index.shape[0]
    paths = path_weights.shape[1]
    share = paths // rows
    own = train // rows
    window = x_window.shape[1]
    counts = point_counts(batch_index, lax.axis_index("col") * train, train)
    coeffs = sine_coeffs((2.0 / (frequencies.shape[1] * col_count)) ** 0.5)
    vmem = pl.BlockSpec(memory_space=pltpu.VMEM)
    dma = pltpu.SemaphoreType.DMA
    hop_shape = (steps, 2, rows // 4, 2)
    alpha, velocity, prior = pl.pallas_call(
        functools.partial(fused_kernel, coeffs, steps, rows),
        in_specs=[vmem] * 10,
        out_specs=[vmem] * 3,
        out_shape=(
            jax.ShapeDtypeStruct((share, train), jnp.float32),
            jax.ShapeDtypeStruct((share, train), jnp.float32),
            jax.ShapeDtypeStruct((paths // 2, window), jnp.float32),
        ),
        scratch_shapes=[
            pltpu.VMEM((steps, paths, train), jnp.bfloat16),
            pltpu.VMEM((2 * own, train), jnp.bfloat16),
            pltpu.VMEM((paths, 2 * own), jnp.float32),
            pltpu.VMEM((2, x_train.shape[0], own), jnp.bfloat16),
            pltpu.VMEM((2 * own, x_train.shape[0]), jnp.float32),
            pltpu.VMEM((share, train), jnp.float32),
            pltpu.VMEM((steps - 1, paths, 2 * own), jnp.float32),
            pltpu.VMEM((steps - 1, 2, share, train), jnp.float32),
            pltpu.VMEM((paths, 2 * own), jnp.bfloat16),
            pltpu.VMEM((2, share, train), jnp.bfloat16),
            pltpu.VMEM((2, paths // 2, window // 2), jnp.bfloat16),
            pltpu.VMEM((2, paths // 2, window // 2), jnp.bfloat16),
            dma(hop_shape), dma(hop_shape), dma(hop_shape), dma(hop_shape),
            dma((steps, 2 * rows)), dma((steps, 2 * rows)),
            dma((steps + 3,)), dma((steps + 3,)),
        ],
        compiler_params=pltpu.CompilerParams(
            collective_id=0, has_side_effects=True, vmem_limit_bytes=48 * 1024 * 1024
        ),
    )(
        x_train, targets[None, :], noise_draws.T, alpha_init.T, velocity_init.T, frequencies,
        phases[None, :], path_weights.T, x_window, counts,
    )
    return alpha.T, velocity.T, prior


def solution(mesh):
    def body(*args):
        share = args[7].shape[1] // mesh.shape["row"]
        fits = share % 16 == 0 and mesh.shape["col"] == 2 and mesh.shape["row"] % 4 == 0
        return (fused_shards if fits and args[9].shape[0] >= 3 else shards)(*args)

    placed = (
        P(None, "col"),
        P("col"),
        P("col", "row"),
        P("col", "row"),
        P("col", "row"),
        P(None, "col"),
        P("col"),
        P("col", None),
        P(None, "row"),
        P(),
    )
    return jax.shard_map(
        body,
        mesh=mesh,
        in_specs=placed,
        out_specs=(P("col", "row"), P("col", "row"), P("col", "row")),
        check_vma=False,
    )
```

```python
import functools

import jax
import jax.numpy as jnp
import numpy as np
from jax import lax
from jax.experimental import pallas as pl
from jax.experimental.pallas import tpu as pltpu
from jax.sharding import PartitionSpec as P

SQRT_THREE = 1.7320508075688772
LENGTH = 1.15
NOISE_VAR = 0.25
MOMENTUM = 0.9
STEP_SIZE = 0.5


def sine_coeffs(scale):
    nodes = 5
    k = np.arange(nodes)
    v = (np.cos((2 * k + 1) * np.pi / (2 * nodes)) + 1) / 2 / 16
    z = np.sqrt(v)
    q = np.sin(2 * np.pi * z) / z
    return [float(c * scale) for c in np.linalg.solve(np.vander(v, nodes, increasing=True), q)]


def scaled_cos(turns, coeffs):
    z = 0.25 - jnp.abs(turns - jnp.round(turns))
    v = z * z
    q = coeffs[-1]
    for c in coeffs[-2::-1]:
        q = q * v + c
    return q * z


def prior_kernel(coeffs, tile_f, freq_ref, phase_ref, weight_ref, point_ref, out_ref):
    feat = freq_ref.shape[0]
    points = point_ref[...]

    def body(i, acc):
        rows = pl.ds(pl.multiple_of(i * tile_f, tile_f), tile_f)
        arg = jnp.dot(freq_ref[rows, :], points, preferred_element_type=jnp.float32)
        turns = (arg + phase_ref[rows, :]) * (0.5 / np.pi)
        phi = scaled_cos(turns, coeffs).astype(jnp.bfloat16)
        return acc + lax.dot_general(
            weight_ref[rows, :], phi, (((0,), (0,)), ((), ())), preferred_element_type=jnp.float32
        )

    out_ref[...] = lax.fori_loop(0, feat // tile_f, body, jnp.zeros(out_ref.shape, jnp.float32))


def prior_sums(freq_t, phase_col, weights, points, total_feat):
    feat, d_in = freq_t.shape
    paths = weights.shape[1]
    n = points.shape[1]
    tile_n = min(512, n)
    coeffs = sine_coeffs((2.0 / total_feat) ** 0.5)
    return pl.pallas_call(
        functools.partial(prior_kernel, coeffs, min(256, feat)),
        grid=(n // tile_n,),
        in_specs=[
            pl.BlockSpec((feat, d_in), lambda i: (0, 0)),
            pl.BlockSpec((feat, 1), lambda i: (0, 0)),
            pl.BlockSpec((feat, paths), lambda i: (0, 0)),
            pl.BlockSpec((d_in, tile_n), lambda i: (0, i)),
        ],
        out_specs=pl.BlockSpec((paths, tile_n), lambda i: (0, i)),
        out_shape=jax.ShapeDtypeStruct((paths, n), jnp.float32),
        cost_estimate=pl.CostEstimate(
            flops=2 * feat * n * (paths + d_in), bytes_accessed=4 * paths * n, transcendentals=feat * n
        ),
    )(freq_t, phase_col, weights, points)


def matern(points, train):
    inner = lax.dot_general(
        train, points, (((0,), (0,)), ((), ())), preferred_element_type=jnp.float32
    )
    point_norm = jnp.sum(jnp.square(points.astype(jnp.float32)), axis=0)
    train_norm = jnp.sum(jnp.square(train.astype(jnp.float32)), axis=0)
    dist_sq = jnp.maximum(train_norm[:, None] + point_norm[None, :] - 2.0 * inner, 0.0)
    scaled = SQRT_THREE / LENGTH * jnp.sqrt(dist_sq)
    return ((1.0 + scaled) * jnp.exp(-scaled)).astype(jnp.bfloat16)


def point_counts(index, start, count):
    lanes = 128
    local = index - start
    high = (local // lanes)[:, None, :] == lax.broadcasted_iota(
        jnp.int32, (1, count // lanes, 1), 1
    )
    low = (local % lanes)[:, None, :] == lax.broadcasted_iota(jnp.int32, (1, lanes, 1), 1)
    tables = lax.dot_general(
        high.astype(jnp.bfloat16),
        low.astype(jnp.bfloat16),
        (((2,), (2,)), ((0,), (0,))),
        preferred_element_type=jnp.float32,
    )
    return tables.reshape(index.shape[0], count)


def shards(
    x_train,
    targets,
    noise_draws,
    alpha_init,
    velocity_init,
    frequencies,
    phases,
    path_weights,
    x_window,
    batch_index,
):
    row_count = lax.axis_size("row")
    col_count = lax.axis_size("col")
    row_id = lax.axis_index("row")
    col_id = lax.axis_index("col")
    train_cols = x_train.shape[1]
    own = train_cols // row_count
    steps = batch_index.shape[0]
    total_feat = frequencies.shape[1] * col_count

    mine = lax.dynamic_slice_in_dim(x_train, row_id * own, own, 1)
    points = lax.all_gather(mine, "col", axis=1, tiled=True)
    freq_t = frequencies.T
    phase_col = phases[:, None]
    kernel_tile = matern(points, x_train)
    prior_rows = prior_sums(freq_t, phase_col, path_weights, points, total_feat)
    window = prior_sums(freq_t, phase_col, path_weights, x_window, total_feat)
    prior_window = lax.psum_scatter(window, "col", scatter_dimension=0, tiled=True)

    counts = point_counts(batch_index, col_id * train_cols, train_cols)
    base = (noise_draws - targets[:, None]).T
    dual, velocity = alpha_init.T, velocity_init.T
    for step in range(steps):
        coeffs = lax.all_gather(dual.astype(jnp.bfloat16), "row", axis=0, tiled=True)
        sums = jnp.dot(coeffs, kernel_tile, preferred_element_type=jnp.float32) + prior_rows
        mine_sums = lax.psum_scatter(sums, "col", scatter_dimension=1, tiled=True)
        arrived = lax.all_to_all(mine_sums, "row", split_axis=0, concat_axis=1, tiled=True)
        gradient = counts[step][None, :] * (arrived + NOISE_VAR * dual + base)
        velocity = MOMENTUM * velocity - STEP_SIZE * gradient
        dual = dual + velocity
    return (dual.T, velocity.T, prior_window)


MESH = pl.DeviceIdType.MESH


def fused_kernel(
    scale_coeffs, steps, rows, x_ref, target_ref, noise_ref, alpha_in, velocity_in, freq_ref,
    phase_ref, weight_ref, window_ref, index_ref, alpha_ref, velocity_ref, prior_ref,
    count_ref, gathered, tile, train_prior, points, points_t, base, outboxes, arrivals, last_outbox, last_arrived,
    window_out, window_in,
    ring_send, ring_recv, pair_send, pair_recv, sum_send, sum_recv, misc_send, misc_recv,
):
    div, rem = lax.div, lax.rem
    row = lax.axis_index("row")
    col = lax.axis_index("col")
    peer = 1 - col
    devices = rows * 2
    flat = row * 2 + col
    paths = weight_ref.shape[0]
    share = paths // rows
    train = x_ref.shape[1]
    own = train // rows
    feat = freq_ref.shape[1]
    half = train // 2
    chips = rows // 2
    core = rem(row, 2)
    chip = div(row, 2)
    depth, side = div(chip, 2), rem(chip, 2)
    place = depth * (1 - side) + (chips - 1 - depth) * side

    def row_at(position, on_core):
        p = rem(position + 2 * chips, chips)
        back = div(p, chips // 2)
        return ((1 - back) * 2 * p + back * (2 * (chips - 1 - p) + 1)) * 2 + on_core

    def device(d):
        other = rem(flat + d, devices)
        return div(other, 2), rem(other, 2)

    barrier = pltpu.get_barrier_semaphore()

    def greet(d, carry):
        pl.semaphore_signal(barrier, inc=1, device_id=device(d), device_id_type=MESH)
        return carry

    lax.fori_loop(1, devices, greet, 0)

    def block(step, r, h):
        return gathered.at[
            step, pl.ds(pl.multiple_of(r * share, share), share), pl.ds(h * half, half)
        ]

    def whole_block(step, r):
        return gathered.at[step, pl.ds(pl.multiple_of(r * share, share), share), :]

    def ring_copy(step, way, k, h):
        sign = 1 - 2 * way
        ref = block(step, row_at(place - sign * k, core), h)
        return pltpu.make_async_remote_copy(
            src_ref=ref, dst_ref=ref,
            send_sem=ring_send.at[step, way, k, h], recv_sem=ring_recv.at[step, way, k, h],
            device_id=(row_at(place + sign, core), col), device_id_type=MESH,
        )

    def pair_copy(step, way, k, h):
        sign = 1 - 2 * way
        ref = block(step, row_at(place - sign * (k + 1), core), h)
        return pltpu.make_async_remote_copy(
            src_ref=ref, dst_ref=ref,
            send_sem=pair_send.at[step, way, k, h], recv_sem=pair_recv.at[step, way, k, h],
            device_id=(row + 1 - 2 * core, col), device_id_type=MESH,
        )

    def own_copy(step):
        ref = whole_block(step, row)
        return pltpu.make_async_remote_copy(
            src_ref=ref, dst_ref=ref,
            send_sem=misc_send.at[step], recv_sem=misc_recv.at[step],
            device_id=(row + 1 - 2 * core, col), device_id_type=MESH,
        )

    last = chips // 2 - 1

    def hops(action):
        def event(e, carry):
            k, h = div(e, 2), rem(e, 2)
            for way in (0, 1):
                @pl.when((k < last) | (h == way))
                def _():
                    action(way, k, h)
            return carry

        lax.fori_loop(0, 2 * (last + 1), event, 0)

    def gather(step, compute):
        gathered[step, pl.ds(pl.multiple_of(row * share, share), share), :] = alpha_ref[
            ...
        ].astype(jnp.bfloat16)
        for h in (0, 1):
            for way in (0, 1):
                ring_copy(step, way, 0, h).start()
        own_copy(step).start()

        def event(e, carry):
            compute(e)
            k, h = div(e, 2), rem(e, 2)
            for way in (0, 1):
                @pl.when((k < last) | (h == way))
                def _():
                    ring_copy(step, way, k, h).wait_recv()

                    @pl.when((k < last - 1) | ((k == last - 1) & (h == way)))
                    def _():
                        ring_copy(step, way, k + 1, h).start()

                    pair_copy(step, way, k, h).start()
            return carry

        lax.fori_loop(0, 2 * (last + 1), event, 0)
        own_copy(step).wait_recv()
        hops(lambda way, k, h: pair_copy(step, way, k, h).wait_recv())

    def boxes(step):
        if step < steps - 1:
            return outboxes.at[step], arrivals.at[step]
        return last_outbox, last_arrived

    def sum_copy(step, d):
        r, c = device(d)
        outbox, arrived = boxes(step)
        return pltpu.make_async_remote_copy(
            src_ref=outbox.at[
                pl.ds(pl.multiple_of(r * share, share), share),
                pl.ds(pl.multiple_of(c * own, own), own),
            ],
            dst_ref=arrived.at[col, :, pl.ds(pl.multiple_of(row * own, own), own)],
            send_sem=sum_send.at[step, d], recv_sem=sum_recv.at[step, d],
            device_id=(r, c), device_id_type=MESH,
        )

    def point_copy():
        return pltpu.make_async_remote_copy(
            src_ref=x_ref.at[:, pl.ds(pl.multiple_of(row * own, own), own)],
            dst_ref=points.at[col],
            send_sem=misc_send.at[steps], recv_sem=misc_recv.at[steps],
            device_id=(row, peer), device_id_type=MESH,
        )

    def window_copy(part):
        width = window_out.shape[2]
        return pltpu.make_async_remote_copy(
            src_ref=window_out.at[part], dst_ref=window_in.at[part],
            send_sem=misc_send.at[steps + 1 + part], recv_sem=misc_recv.at[steps + 1 + part],
            device_id=(row, peer), device_id_type=MESH,
        )

    alpha_ref[...] = alpha_in[...]
    velocity_ref[...] = velocity_in[...]
    base[...] = noise_ref[...] - target_ref[...]
    pl.semaphore_wait(barrier, devices - 1)
    point_copy().start()
    points[col] = x_ref[:, pl.ds(pl.multiple_of(row * own, own), own)]
    train_prior[...] = jnp.zeros_like(train_prior)
    events = 2 * (last + 1)

    def phi_block(pts_t, cols):
        arg = jnp.dot(pts_t, freq_ref[:, cols], preferred_element_type=jnp.float32)
        turns = (arg + phase_ref[:, cols]) * (0.5 / np.pi)
        return scaled_cos(turns, scale_coeffs).astype(jnp.bfloat16)

    def against(a, b):
        return lax.dot_general(
            a, b, (((1,), (1,)), ((), ())), preferred_element_type=jnp.float32
        )

    def train_work(e):
        @pl.when(e == 0)
        def _():
            point_copy().wait_recv()
            for c in (0, 1):
                points_t[c * own : (c + 1) * own, :] = points[c].astype(jnp.float32).T

        width = train // events
        cols = pl.ds(pl.multiple_of(e * width, width), width)
        trains = x_ref[:, cols]
        train_norm = jnp.sum(jnp.square(trains.astype(jnp.float32)), axis=0, keepdims=True)
        fwidth = feat // events
        fcols = pl.ds(pl.multiple_of(e * fwidth, fwidth), fwidth)
        group = 128

        def rows_of(i, carry):
            span = pl.ds(pl.multiple_of(i * group, group), group)
            pts = points_t[span, :]
            pts_norm = jnp.sum(jnp.square(pts), axis=1, keepdims=True)
            pts = pts.astype(jnp.bfloat16)
            inner = jnp.dot(pts, trains, preferred_element_type=jnp.float32)
            dist_sq = jnp.maximum(pts_norm + train_norm - 2.0 * inner, 0.0)
            scaled = SQRT_THREE / LENGTH * jnp.sqrt(dist_sq)
            tile[span, cols] = ((1.0 + scaled) * jnp.exp(-scaled)).astype(jnp.bfloat16)
            train_prior[:, span] += against(weight_ref[:, fcols], phi_block(pts, fcols))
            return carry

        lax.fori_loop(0, 2 * own // group, rows_of, 0)

    def count_points(step):
        lanes = 128
        local = index_ref[step : step + 1, :] - col * train
        high_ids = lax.broadcasted_iota(jnp.int32, (train // lanes, 1), 0)
        low_ids = lax.broadcasted_iota(jnp.int32, (lanes, 1), 0)
        high = ((local >> 7) == high_ids).astype(jnp.float32).astype(jnp.bfloat16)
        low = ((local & 127) == low_ids).astype(jnp.float32).astype(jnp.bfloat16)
        table = against(high, low)
        for i in range(train // lanes):
            count_ref[step : step + 1, i * lanes : (i + 1) * lanes] = table[i : i + 1, :]

    tiles = 2 * events
    wide = window_ref.shape[1] // tiles

    def window_work(part):
        def work(e):
            span = pl.ds(pl.multiple_of((part * events + e) * wide, wide), wide)
            pts = window_ref[:, span].astype(jnp.float32).T.astype(jnp.bfloat16)
            fwidth = min(512, feat)

            def feats(i, acc):
                fcols = pl.ds(pl.multiple_of(i * fwidth, fwidth), fwidth)
                return acc + against(weight_ref[:, fcols], phi_block(pts, fcols))

            acc = lax.fori_loop(
                0, feat // fwidth, feats, jnp.zeros((paths, wide), jnp.float32)
            )
            kept = paths // 2
            mine = jnp.where(col == 0, acc[:kept], acc[kept:])
            sent = jnp.where(col == 0, acc[kept:], acc[:kept])
            prior_ref[:, span] = mine
            window_out[part, :, pl.ds(pl.multiple_of(e * wide, wide), wide)] = sent.astype(
                jnp.bfloat16
            )

        return work

    for step in range(steps):
        if step == 0:
            gather(step, train_work)
        elif step < 3:
            gather(step, window_work(step - 1))
            window_copy(step - 1).start()
        else:
            gather(step, lambda e: None)
        outbox, arrived = boxes(step)
        for c in (0, 1):
            span = slice(c * own, (c + 1) * own)
            sums = against(gathered[step], tile[span, :]) + train_prior[:, span]
            outbox[:, span] = sums.astype(outbox.dtype)

        def send(d, carry):
            sum_copy(step, d).start()
            return carry

        lax.fori_loop(1, devices, send, 0)
        arrived[col, :, pl.ds(pl.multiple_of(row * own, own), own)] = outbox[
            pl.ds(pl.multiple_of(row * share, share), share),
            pl.ds(pl.multiple_of(col * own, own), own),
        ]

        count_points(step)

        def receive(d, carry):
            sum_copy(step, d).wait_recv()
            return carry

        lax.fori_loop(1, devices, receive, 0)
        total = arrived[0].astype(jnp.float32) + arrived[1].astype(jnp.float32)
        alpha = alpha_ref[...]
        gradient = count_ref[step : step + 1, :] * (total + NOISE_VAR * alpha + base[...])
        speed = MOMENTUM * velocity_ref[...] - STEP_SIZE * gradient
        velocity_ref[...] = speed
        alpha_ref[...] = alpha + speed

    for part in (0, 1):
        window_copy(part).wait()
        width = window_out.shape[2]
        span = slice(part * width, (part + 1) * width)
        prior_ref[:, span] = prior_ref[:, span] + window_in[part].astype(jnp.float32)
    point_copy().wait_send()
    for step in range(steps):
        own_copy(step).wait_send()
        hops(lambda way, k, h: ring_copy(step, way, k, h).wait_send())
        hops(lambda way, k, h: pair_copy(step, way, k, h).wait_send())

        def drain(d, carry):
            sum_copy(step, d).wait_send()
            return carry

        lax.fori_loop(1, devices, drain, 0)


def fused_shards(
    x_train, targets, noise_draws, alpha_init, velocity_init, frequencies, phases, path_weights,
    x_window, batch_index,
):
    rows = lax.axis_size("row")
    col_count = lax.axis_size("col")
    train = x_train.shape[1]
    steps = batch_index.shape[0]
    paths = path_weights.shape[1]
    share = paths // rows
    own = train // rows
    window = x_window.shape[1]
    coeffs = sine_coeffs((2.0 / (frequencies.shape[1] * col_count)) ** 0.5)
    vmem = pl.BlockSpec(memory_space=pltpu.VMEM)
    dma = pltpu.SemaphoreType.DMA
    hop_shape = (steps, 2, rows // 4, 2)
    alpha, velocity, prior = pl.pallas_call(
        functools.partial(fused_kernel, coeffs, steps, rows),
        in_specs=[vmem] * 10,
        out_specs=[vmem] * 3,
        out_shape=(
            jax.ShapeDtypeStruct((share, train), jnp.float32),
            jax.ShapeDtypeStruct((share, train), jnp.float32),
            jax.ShapeDtypeStruct((paths // 2, window), jnp.float32),
        ),
        scratch_shapes=[
            pltpu.VMEM((steps, train), jnp.float32),
            pltpu.VMEM((steps, paths, train), jnp.bfloat16),
            pltpu.VMEM((2 * own, train), jnp.bfloat16),
            pltpu.VMEM((paths, 2 * own), jnp.float32),
            pltpu.VMEM((2, x_train.shape[0], own), jnp.bfloat16),
            pltpu.VMEM((2 * own, x_train.shape[0]), jnp.float32),
            pltpu.VMEM((share, train), jnp.float32),
            pltpu.VMEM((steps - 1, paths, 2 * own), jnp.float32),
            pltpu.VMEM((steps - 1, 2, share, train), jnp.float32),
            pltpu.VMEM((paths, 2 * own), jnp.bfloat16),
            pltpu.VMEM((2, share, train), jnp.bfloat16),
            pltpu.VMEM((2, paths // 2, window // 2), jnp.bfloat16),
            pltpu.VMEM((2, paths // 2, window // 2), jnp.bfloat16),
            dma(hop_shape), dma(hop_shape), dma(hop_shape), dma(hop_shape),
            dma((steps, 2 * rows)), dma((steps, 2 * rows)),
            dma((steps + 3,)), dma((steps + 3,)),
        ],
        compiler_params=pltpu.CompilerParams(
            collective_id=0, has_side_effects=True, vmem_limit_bytes=48 * 1024 * 1024
        ),
    )(
        x_train, targets[None, :], noise_draws.T, alpha_init.T, velocity_init.T, frequencies,
        phases[None, :], path_weights.T, x_window, batch_index,
    )
    return alpha.T, velocity.T, prior


def solution(mesh):
    def body(*args):
        share = args[7].shape[1] // mesh.shape["row"]
        fits = share % 16 == 0 and mesh.shape["col"] == 2 and mesh.shape["row"] % 4 == 0
        return (fused_shards if fits and args[9].shape[0] >= 3 else shards)(*args)

    placed = (
        P(None, "col"),
        P("col"),
        P("col", "row"),
        P("col", "row"),
        P("col", "row"),
        P(None, "col"),
        P("col"),
        P("col", None),
        P(None, "row"),
        P(),
    )
    return jax.shard_map(
        body,
        mesh=mesh,
        in_specs=placed,
        out_specs=(P("col", "row"), P("col", "row"), P("col", "row")),
        check_vma=False,
    )
```
